32 devices in a mesh: tile: 4 (over z), wide: 8 (over y, x, core).
Axes of the slice: x: 2, y: 2, z: 4, core: 2. Of those that a mesh axis runs over, the one named last changes fastest.
Arguments:
- coords: float32 [192, 2, 128], P(('tile', 'wide')), may hold values from 0 to 1, as said below
- fields: float32 [192, 4, 128], P(('tile', 'wide')), may hold values from -6 to 6
- counts: int32 [4, 8], P('tile'), may hold values from 1 to 6, as said below
- place: int32 [128], replicated, may hold values from 0 to 191, as said below
- neighbours: int32 [192, 3], P('tile'), may hold values from -1 to 127, as said below
Outputs:
- whitened: float32 [192, 4, 128], P(('tile', 'wide'))
- logdet: float32 [192], P(('tile', 'wide'))
The draws below stay inside these ranges and needn't reach their ends.
Inputs may be any that keep to these rules, and one draw needn't show every extreme that they name: `coords`: each slot's points lie around a centre of its own; the slots of one tile have their centres in one strip of the first coordinate, tiles in order. `counts`: the live blocks of one tile number 4 times its devices; in every tile some device has 6. `place`: names every live slot exactly once. `neighbours`: entries of a live slot name distinct blocks of smaller ordinal whose slots lie in the same tile or the tile before; -1 marks an empty entry; every entry of a slot that is not live is -1.
All inputs are finite; a program needn't handle non-finite values.
Results may differ from the reference program's by a relative error of at most 0.0003.
Values sent between devices are 32-bit elements; how exact they have to be, the bound alone decides.
No kernel may reach another device: no remote copies, remote signals or barrier semaphores. Data moves between devices by JAX's collectives and lax.ppermute only.
A program may use at most 64 MiB of HBM per device.

```python
import math
import jax
import jax.numpy as jnp
from jax import lax

B = 128
K = 3
LIVE = 4
CAP = 6
SLOTS = 192
NBLK = 128
N_TILE = 4
N_WIDE = 8


def centres(key):
    key_x, key_y = jax.random.split(jax.random.fold_in(key, 11), 2)
    strip = 1024 // N_TILE
    slot_tile = jnp.arange(SLOTS, dtype=jnp.int32) // (CAP * N_WIDE)
    centre_x = slot_tile * strip + jax.random.randint(key_x, (SLOTS,), 0, strip)
    centre_y = jax.random.randint(key_y, (SLOTS,), 0, 1024)
    return (centre_x.astype(jnp.int32), centre_y.astype(jnp.int32))


def layout(key):
    key_pair, key_shift, key_shuffle = jax.random.split(jax.random.fold_in(key, 7), 3)
    device_count = N_TILE * N_WIDE
    pair_order = jax.vmap(lambda one_key: jax.random.permutation(one_key, N_WIDE))(jax.random.split(key_pair, N_TILE))
    shift_size = jax.random.randint(key_shift, (N_TILE, N_WIDE // 2), 0, LIVE - 1)
    shift_size = shift_size.at[:, 0].set(LIVE - 2)
    paired = jnp.stack([LIVE + shift_size, LIVE - shift_size], axis=2).reshape(N_TILE, N_WIDE)
    tile_rows = jnp.arange(N_TILE, dtype=jnp.int32)[:, None]
    counts = jnp.zeros((N_TILE, N_WIDE), jnp.int32).at[tile_rows, pair_order].set(paired.astype(jnp.int32))
    slot_live = (jnp.arange(CAP, dtype=jnp.int32)[None, :] < counts.reshape(device_count)[:, None]).reshape(SLOTS)
    shuffled = jax.random.permutation(key_shuffle, SLOTS).astype(jnp.int32)
    dead_flags = 1 - slot_live[shuffled].astype(jnp.int32)
    place = shuffled[jnp.argsort(dead_flags, stable=True)][:NBLK].astype(jnp.int32)
    ordinal = jnp.full((SLOTS,), -1, jnp.int32).at[place].set(jnp.arange(NBLK, dtype=jnp.int32))
    slot_tile = jnp.arange(SLOTS, dtype=jnp.int32) // (CAP * N_WIDE)
    block_tile = place // (CAP * N_WIDE)
    nearby = (block_tile[None, :] == slot_tile[:, None]) | (block_tile[None, :] == slot_tile[:, None] - 1)
    earlier = jnp.arange(NBLK, dtype=jnp.int32)[None, :] < ordinal[:, None]
    centre_x, centre_y = centres(key)
    delta_x = centre_x[:, None] - centre_x[place][None, :]
    delta_y = centre_y[:, None] - centre_y[place][None, :]
    squared = (delta_x * delta_x + delta_y * delta_y) // 32
    scores = (65537 - squared) * NBLK + (NBLK - 1 - jnp.arange(NBLK, dtype=jnp.int32))[None, :]
    scores = jnp.where(nearby & earlier, scores, -1)
    best_scores, best_index = lax.top_k(scores, K)
    neighbours = jnp.where(best_scores >= 0, best_index, -1).astype(jnp.int32)
    return (counts, place, neighbours)


def draw_coords(key, part):
    centre_x, centre_y = centres(key)
    middle = (jnp.stack([centre_x, centre_y], axis=1).astype(jnp.float32) + 0.5) / 1024.0
    offset = jnp.clip(0.1 * jax.random.normal(jax.random.fold_in(key, 13), (SLOTS, 2, B), jnp.float32), -0.3, 0.3)
    return jnp.clip(middle[:, :, None] + offset, 0.0, 1.0)


def draw_counts(key, part):
    return layout(key)[0]


def draw_place(key, part):
    return layout(key)[1]


def draw_neighbours(key, part):
    return layout(key)[2]


def block_scale(stream_key, shape, cuts, smallest, top_value):
    factor_of = 1.0
    for axis_at, parts in cuts:
        heights = jax.random.uniform(jax.random.fold_in(jax.random.fold_in(stream_key, 6), axis_at), (parts,), jnp.float32, smallest / len(cuts), top_value / len(cuts))
        factor_of = factor_of * jnp.repeat(jnp.exp(heights), shape[axis_at] // parts).reshape((-1,) + (1,) * (len(shape) - 1 - axis_at))
    return factor_of


def scatter_about(own_key, extent, width, most, cuts=(), kind=jnp.bfloat16):
    entries = width * jax.random.normal(own_key, extent, jnp.float32)
    if cuts:
        entries = entries * block_scale(own_key, extent, cuts, -0.22, 0.18)
    return jnp.clip(entries, -most, most).astype(kind)


def setup_inputs(seed: int = 0) -> dict:
    seeds = jax.random.split(jax.random.key(seed), 6)
    return {
        "coords": draw_coords(jax.random.fold_in(seeds[5], 71), 0),
        "fields": scatter_about(seeds[1], (SLOTS, 4, B), 1.0, 6.0, ((0, 32),), jnp.float32),
        "counts": draw_counts(jax.random.fold_in(seeds[5], 71), 0),
        "place": draw_place(jax.random.fold_in(seeds[5], 71), 0),
        "neighbours": draw_neighbours(jax.random.fold_in(seeds[5], 71), 0),
    }


length_scale = 0.08
nugget = 0.25
root_three = math.sqrt(3.0)

def kernel(sites_left, sites_right):
    delta_x = sites_left[0][:, None] - sites_right[0][None, :]
    delta_y = sites_left[1][:, None] - sites_right[1][None, :]
    scaled = root_three / length_scale * jnp.sqrt(delta_x * delta_x + delta_y * delta_y)
    return (1.0 + scaled) * jnp.exp(-scaled)

def whiten(own_block, near_blocks, is_valid):
    weight_mask = jnp.repeat(is_valid.astype(jnp.float32), B)
    near_sites = jnp.transpose(near_blocks[:, :2, :], (1, 0, 2)).reshape(2, K * B)
    near_values = jnp.transpose(near_blocks[:, 2:, :], (1, 0, 2)).reshape(4, K * B) * weight_mask[None, :]
    cov_near = kernel(near_sites, near_sites) * weight_mask[:, None] * weight_mask[None, :]
    cov_near = cov_near + jnp.diag(nugget + 1.0 - weight_mask)
    cov_cross = kernel(own_block[:2], near_sites) * weight_mask[None, :]
    cov_own = kernel(own_block[:2], own_block[:2]) + nugget * jnp.eye(B, dtype=jnp.float32)
    chol_near = jnp.linalg.cholesky(cov_near)
    right_sides = jnp.concatenate([cov_cross.T, near_values.T], axis=1)
    solved = jax.scipy.linalg.solve_triangular(chol_near, right_sides, lower=True)
    factor = solved[:, :B]
    reduced = solved[:, B:]
    cov_cond = cov_own - jnp.dot(factor.T, factor, precision=lax.Precision.HIGHEST)
    cond_mean = jnp.dot(factor.T, reduced, precision=lax.Precision.HIGHEST)
    chol_cond = jnp.linalg.cholesky(cov_cond)
    result = jax.scipy.linalg.solve_triangular(chol_cond, own_block[2:].T - cond_mean, lower=True)
    return (result.T, 2.0 * jnp.sum(jnp.log(jnp.diagonal(chol_cond))))

def reference(coords, fields, counts, place, neighbours):
    blocks = jnp.concatenate([coords, fields], axis=1)
    live_mask = (jnp.arange(CAP, dtype=jnp.int32)[None, :] < counts.reshape(-1)[:, None]).astype(jnp.float32)

    def per_device(group_index):
        first_row = (group_index * CAP).astype(jnp.int32)
        own_blocks = lax.dynamic_slice_in_dim(blocks, first_row, CAP, 0)
        listed = lax.dynamic_slice_in_dim(neighbours, first_row, CAP, 0)
        near_blocks = blocks[place[jnp.maximum(listed, 0)]]
        return jax.vmap(whiten)(own_blocks, near_blocks, listed >= 0)
    result, log_terms = lax.map(per_device, jnp.arange(SLOTS // CAP, dtype=jnp.int32))
    result = result * live_mask[:, :, None, None]
    log_terms = log_terms * live_mask
    return (result.reshape(SLOTS, 4, B), log_terms.reshape(SLOTS))
```

```python
import math

import jax
import jax.numpy as jnp
from jax import lax
from jax.experimental import pallas as pl
from jax.experimental.pallas import tpu as pltpu
from jax.sharding import PartitionSpec as P

B = 128
K = 3
NB = K + 1
SUB = 8
PANEL = 16
GROUP = 8

length_scale = 0.08
nugget = 0.25
root_three = math.sqrt(3.0)

f32 = jnp.float32
bf16 = jnp.bfloat16


def split(a):
    high = a.astype(bf16)
    return high, (a - high.astype(f32)).astype(bf16)


def product(a, b, contract):
    def dot(x, y):
        return lax.dot_general(x, y, (contract, ((), ())), preferred_element_type=f32)

    return dot(a[0], b[0]) + (dot(a[0], b[1]) + dot(a[1], b[0]))


def column(v, at):
    return jnp.broadcast_to(v[:, at : at + 1], v.shape)


def eliminate(rows, first, lane):
    n = len(rows)
    lower = {}
    pivots = []
    inverse = []
    for g in range(0, n, GROUP):
        cols = {}
        for s in range(g, g + GROUP):
            for i in range(s, n):
                cols[i, s] = column(rows[i], first + s)
        for t in range(g, g + GROUP):
            pivot = cols[t, t]
            inv = 1.0 / pivot
            pivots.append(pivot)
            inverse.append(inv)
            lead = jnp.where(lane == first + t, 1.0 + pivot, rows[t])
            for i in range(t + 1, n):
                lower[i, t] = cols[i, t] * inv
                for u in range(t + 1, min(g + GROUP, i + 1)):
                    cols[i, u] = cols[i, u] - lower[i, t] * cols[u, t]
                rows[i] = rows[i] - lower[i, t] * lead
    inside = (lane >= first) & (lane < first + n)
    clean = []
    for t in range(n):
        row = jnp.where(inside & (lane > first + t), 0.0, rows[t])
        clean.append(jnp.where(lane == first + t, 1.0, row))
    back = [clean[t] * inverse[t] for t in range(n)]
    for t in range(n - 1, 0, -1):
        for i in range(t):
            back[i] = back[i] - lower[t, i] * back[t]
    return clean, pivots, back


def whiten_kernel(
    n_wide, slots, counts_ref, place_ref, near_ref, coords_ref, fields_ref, table_ref,
    out_ref, logdet_ref, cov, weight, sites, sites_t, rhs, swept,
):
    tile_index = lax.axis_index("tile")
    wide_index = lax.axis_index("wide")
    lane = lax.broadcasted_iota(jnp.int32, (SUB, B), 1)

    sites[...] = jnp.zeros_like(sites)
    rhs[...] = jnp.zeros_like(rhs)
    valid = {}
    for m in range(slots):
        for k in range(K):
            listed = near_ref[wide_index * slots + m, k]
            valid[m, k] = (listed >= 0).astype(f32)
            source = place_ref[jnp.maximum(listed, 0)]
            device = source // slots
            prior = (device // n_wide != tile_index).astype(jnp.int32)
            block = table_ref[device % n_wide, prior, source % slots]
            sites[pl.ds(m * SUB + k, 1), :] = block[0:1]
            sites[pl.ds(m * SUB + NB + k, 1), :] = block[1:2]
            rhs[k, m, 0:4, :] = block[2:6] * valid[m, k]
        sites[pl.ds(m * SUB + K, 1), :] = coords_ref[m, 0:1, :]
        sites[pl.ds(m * SUB + NB + K, 1), :] = coords_ref[m, 1:2, :]
        rhs[K, m, 0:4, :] = fields_ref[m]
        valid[m, K] = 1.0
    sites_t[...] = sites[...].T

    row_id = lax.broadcasted_iota(jnp.int32, (B, B), 0)
    col_id = lax.broadcasted_iota(jnp.int32, (B, B), 1)
    for m in range(slots):
        for c in range(NB):
            at = m * SUB + c
            x_row = jnp.broadcast_to(sites_t[:, at : at + 1], (B, B))
            y_row = jnp.broadcast_to(sites_t[:, at + NB : at + NB + 1], (B, B))
            for r in range(c + 1):
                dx = x_row - sites[pl.ds(m * SUB + r, 1), :]
                dy = y_row - sites[pl.ds(m * SUB + NB + r, 1), :]
                squared = dx * dx + dy * dy
                scaled = squared * (root_three / length_scale * lax.rsqrt(jnp.maximum(squared, 1e-30)))
                value = (1.0 + scaled) * jnp.exp(-scaled)
                if r < K:
                    value = value * (valid[m, c] * valid[m, r])
                if c == r:
                    value = value + jnp.where(row_id == col_id, nugget + 1.0 - valid[m, c], 0.0)
                cov[c * NB + r, m * B : (m + 1) * B, :] = value

    def block_step(r, dets):
        diag = cov.at[r * NB + r]
        for p in range(0, B, PANEL):
            rows = [diag[pl.ds(p + t, SUB, stride=B), :] for t in range(PANEL)]
            clean, pivots, back = eliminate(rows, p, lane)
            for t in range(PANEL):
                weight[pl.ds(p + t, SUB, stride=B), :] = jnp.where(
                    lane <= p + t, clean[t] * lax.rsqrt(pivots[t]), 0.0)
                dets = jnp.where(lane == p + t, pivots[t], dets)
                swept[pl.ds(t, SUB, stride=PANEL), :] = back[t]
            rest = B - p - PANEL
            if rest == 0:
                continue
            for m in range(slots):
                here = slice(m * B + p + PANEL, (m + 1) * B)
                old = diag[here, :]
                high, low = split(swept[m * PANEL : (m + 1) * PANEL, :])
                pad = lambda q: jnp.concatenate(
                    ([jnp.zeros((p, B), bf16)] if p else []) + [q, jnp.zeros((rest, B), bf16)], axis=0)
                change = product(split(old), (pad(high), pad(low)), ((1,), (0,)))
                ids = lax.broadcasted_iota(jnp.int32, old.shape, 1)
                kept = jnp.where((ids >= p) & (ids < p + PANEL), 0.0, old)
                diag[here, :] = kept - change

        for m in range(slots):
            here = slice(m * B, (m + 1) * B)
            w = split(weight[here, :])
            solved = product(split(rhs[r, m]), w, ((1,), (1,)))
            rhs[r, m] = solved
            solved = split(solved)

            def solve(c, carry):
                x = product(split(cov[c * NB + r, here, :]), w, ((1,), (1,)))
                cov[c * NB + r, here, :] = x
                rhs[c, m] = rhs[c, m] - product(solved, split(x), ((1,), (1,)))
                return carry

            lax.fori_loop(r + 1, NB, solve, 0)

            def update(c, carry):
                x = split(cov[c * NB + r, here, :])

                def one(e, inner):
                    y = split(cov[e * NB + r, here, :])
                    cov[c * NB + e, here, :] = cov[c * NB + e, here, :] - product(x, y, ((1,), (1,)))
                    return inner

                lax.fori_loop(r + 1, c + 1, one, 0)
                return carry

            lax.fori_loop(r + 1, NB, update, 0)
        return dets

    dets = lax.fori_loop(0, NB, block_step, jnp.ones((SUB, B), f32))
    total = jnp.sum(jnp.log(dets), axis=1, keepdims=True)
    live_count = counts_ref[0, wide_index]
    slot_id = lax.broadcasted_iota(jnp.int32, (SUB, 1), 0)
    logdet_ref[...] = jnp.broadcast_to(jnp.where(slot_id < live_count, total, 0.0), (SUB, B))
    for m in range(slots):
        live = (m < live_count).astype(f32)
        out_ref[m] = rhs[K, m, 0:4, :] * live


def local(coords, fields, counts, place, neighbours):
    slots = coords.shape[0]
    n_wide = lax.axis_size("wide")
    n_tile = lax.axis_size("tile")
    blocks = jnp.concatenate([coords, fields], axis=1)
    prior = lax.ppermute(blocks, "tile", [(i, i + 1) for i in range(n_tile - 1)])
    table = lax.all_gather(jnp.stack([blocks, prior]), "wide", axis=0)
    smem = pl.BlockSpec(memory_space=pltpu.SMEM)
    vmem = pl.BlockSpec(memory_space=pltpu.VMEM)
    result, logs = pl.pallas_call(
        lambda *refs: whiten_kernel(n_wide, slots, *refs),
        out_shape=(
            jax.ShapeDtypeStruct((slots, 4, B), f32),
            jax.ShapeDtypeStruct((SUB, B), f32),
        ),
        in_specs=[smem, smem, smem, vmem, vmem, vmem],
        out_specs=(vmem, vmem),
        scratch_shapes=[
            pltpu.VMEM((NB * NB, SUB * B, B), f32),
            pltpu.VMEM((SUB * B, B), f32),
            pltpu.VMEM((B, B), f32),
            pltpu.VMEM((B, B), f32),
            pltpu.VMEM((NB, slots, SUB, B), f32),
            pltpu.VMEM((SUB * PANEL, B), f32),
        ],
        compiler_params=pltpu.CompilerParams(vmem_limit_bytes=48 << 20),
    )(counts, place, neighbours, coords, fields, table)
    return result, logs[:slots, 0]


def solution(mesh):
    in_specs = (
        P(("tile", "wide"), None, None),
        P(("tile", "wide"), None, None),
        P("tile", None),
        P(),
        P("tile", None),
    )
    out_specs = (P(("tile", "wide"), None, None), P(("tile", "wide")))
    return jax.shard_map(local, mesh=mesh, in_specs=in_specs, out_specs=out_specs, check_vma=False)
```

```python
import math

import jax
import jax.numpy as jnp
from jax import lax
from jax.experimental import pallas as pl
from jax.experimental.pallas import tpu as pltpu
from jax.sharding import PartitionSpec as P

B = 128
K = 3
NB = K + 1
SUB = 8
PANEL = 16
GROUP = 8

length_scale = 0.08
nugget = 0.25
root_three = math.sqrt(3.0)

f32 = jnp.float32
bf16 = jnp.bfloat16


def pieces(a):
    first = a.astype(bf16)
    rest = a - first.astype(f32)
    second = rest.astype(bf16)
    return first, second, (rest - second.astype(f32)).astype(bf16)


def left(a):
    first, second, third = pieces(a)
    return jnp.concatenate([first, second], axis=1), jnp.concatenate([first, third], axis=1)


def right_rows(b):
    first, second, third = pieces(b)
    main = jnp.concatenate(
        [jnp.concatenate([first, first], axis=1), jnp.concatenate([second, second], axis=1)], axis=0)
    return main, jnp.concatenate([third, first], axis=1)


def right_cols(b, before, after):
    def pad(q):
        parts = [q]
        if before:
            parts.insert(0, jnp.zeros((before, B), bf16))
        if after:
            parts.append(jnp.zeros((after, B), bf16))
        return jnp.concatenate(parts, axis=0)

    first, second, third = (pad(q) for q in pieces(b))
    row = jnp.concatenate([first, second], axis=1)
    return jnp.concatenate([row, row], axis=0), jnp.concatenate([third, first], axis=0)


def product(a, b, across):
    def dot(x, y):
        return lax.dot_general(x, y, (((1,), (across,)), ((), ())), preferred_element_type=f32)

    wide = dot(a[0], b[0])
    return wide[:, :B] + (wide[:, B:] + dot(a[1], b[1]))


def column(v, at):
    return jnp.broadcast_to(v[:, at : at + 1], v.shape)


def eliminate(rows, first, lane):
    n = len(rows)
    lower = {}
    pivots = []
    inverse = []
    for g in range(0, n, GROUP):
        cols = {}
        for s in range(g, g + GROUP):
            for i in range(s, n):
                cols[i, s] = column(rows[i], first + s)
        for t in range(g, g + GROUP):
            pivot = cols[t, t]
            inv = 1.0 / pivot
            pivots.append(pivot)
            inverse.append(inv)
            lead = jnp.where(lane == first + t, 1.0 + pivot, rows[t])
            for i in range(t + 1, n):
                lower[i, t] = cols[i, t] * inv
                for u in range(t + 1, min(g + GROUP, i + 1)):
                    cols[i, u] = cols[i, u] - lower[i, t] * cols[u, t]
                rows[i] = rows[i] - lower[i, t] * lead
    inside = (lane >= first) & (lane < first + n)
    clean = []
    for t in range(n):
        row = jnp.where(inside & (lane > first + t), 0.0, rows[t])
        clean.append(jnp.where(lane == first + t, 1.0, row))
    back = [clean[t] * inverse[t] for t in range(n)]
    for t in range(n - 1, 0, -1):
        for i in range(t):
            back[i] = back[i] - lower[t, i] * back[t]
    return clean, pivots, back


def whiten_kernel(
    n_wide, slots, counts_ref, place_ref, near_ref, coords_ref, fields_ref, table_ref,
    out_ref, logdet_ref, cov, weight, sites, sites_t, rhs, swept,
):
    tile_index = lax.axis_index("tile")
    wide_index = lax.axis_index("wide")
    lane = lax.broadcasted_iota(jnp.int32, (SUB, B), 1)

    sites[...] = jnp.zeros_like(sites)
    rhs[...] = jnp.zeros_like(rhs)
    valid = {}
    for m in range(slots):
        for k in range(K):
            listed = near_ref[wide_index * slots + m, k]
            valid[m, k] = (listed >= 0).astype(f32)
            source = place_ref[jnp.maximum(listed, 0)]
            device = source // slots
            prior = (device // n_wide != tile_index).astype(jnp.int32)
            block = table_ref[device % n_wide, prior, source % slots]
            sites[pl.ds(m * SUB + k, 1), :] = block[0:1]
            sites[pl.ds(m * SUB + NB + k, 1), :] = block[1:2]
            rhs[k, m, 0:4, :] = block[2:6] * valid[m, k]
        sites[pl.ds(m * SUB + K, 1), :] = coords_ref[m, 0:1, :]
        sites[pl.ds(m * SUB + NB + K, 1), :] = coords_ref[m, 1:2, :]
        rhs[K, m, 0:4, :] = fields_ref[m]
        valid[m, K] = 1.0
    sites_t[...] = sites[...].T

    row_id = lax.broadcasted_iota(jnp.int32, (B, B), 0)
    col_id = lax.broadcasted_iota(jnp.int32, (B, B), 1)
    for m in range(slots):
        for c in range(NB):
            at = m * SUB + c
            x_row = jnp.broadcast_to(sites_t[:, at : at + 1], (B, B))
            y_row = jnp.broadcast_to(sites_t[:, at + NB : at + NB + 1], (B, B))
            for r in range(c + 1):
                dx = x_row - sites[pl.ds(m * SUB + r, 1), :]
                dy = y_row - sites[pl.ds(m * SUB + NB + r, 1), :]
                squared = dx * dx + dy * dy
                scaled = squared * (root_three / length_scale * lax.rsqrt(jnp.maximum(squared, 1e-30)))
                value = (1.0 + scaled) * jnp.exp(-scaled)
                if r < K:
                    value = value * (valid[m, c] * valid[m, r])
                if c == r:
                    value = value + jnp.where(row_id == col_id, nugget + 1.0 - valid[m, c], 0.0)
                cov[r, (m * NB + c) * B : (m * NB + c + 1) * B, :] = value

    def block_step(r, dets):
        mine = cov.at[r]
        start = pl.multiple_of(r * B, B)
        for p in range(0, B, PANEL):
            rows = [mine[pl.ds(start + p + t, SUB, stride=NB * B), :] for t in range(PANEL)]
            clean, pivots, back = eliminate(rows, p, lane)
            for t in range(PANEL):
                weight[pl.ds(p + t, SUB, stride=B), :] = jnp.where(
                    lane <= p + t, clean[t] * lax.rsqrt(pivots[t]), 0.0)
                dets = jnp.where(lane == p + t, pivots[t], dets)
                swept[pl.ds(t, SUB, stride=PANEL), :] = back[t]
            rest = B - p - PANEL
            if rest == 0:
                continue
            ids = lax.broadcasted_iota(jnp.int32, (rest, B), 1)
            for m in range(slots):
                here = pl.ds(start + m * NB * B + p + PANEL, rest)
                old = mine[here, :]
                change = product(left(old), right_cols(swept[m * PANEL : (m + 1) * PANEL, :], p, rest), 0)
                mine[here, :] = jnp.where((ids >= p) & (ids < p + PANEL), 0.0, old) - change

        for at in range(NB):
            pl.when(r == at)(lambda at=at: couple(at))
        return dets

    def couple(r):
        for m in range(slots):
            w = right_rows(weight[m * B : (m + 1) * B, :])
            solved = product(left(rhs[r, m]), w, 1)
            rhs[r, m] = solved
            if r == K:
                continue
            later = (NB - 1 - r) * B
            x = product(left(cov[r, pl.ds((m * NB + r + 1) * B, later), :]), w, 1)
            x_left = left(x)
            z_left = left(solved)
            for e in range(r + 1, NB):
                skip = (e - r - 1) * B
                y = right_rows(x[skip : skip + B])
                here = pl.ds((m * NB + e) * B, later - skip)
                cov[e, here, :] = cov[e, here, :] - product(tuple(q[skip:] for q in x_left), y, 1)
                rhs[e, m] = rhs[e, m] - product(z_left, y, 1)

    dets = lax.fori_loop(0, NB, block_step, jnp.ones((SUB, B), f32))
    total = jnp.sum(jnp.log(dets), axis=1, keepdims=True)
    live_count = counts_ref[0, wide_index]
    slot_id = lax.broadcasted_iota(jnp.int32, (SUB, 1), 0)
    logdet_ref[...] = jnp.broadcast_to(jnp.where(slot_id < live_count, total, 0.0), (SUB, B))
    for m in range(slots):
        live = (m < live_count).astype(f32)
        out_ref[m] = rhs[K, m, 0:4, :] * live


def local(coords, fields, counts, place, neighbours):
    slots = coords.shape[0]
    n_wide = lax.axis_size("wide")
    n_tile = lax.axis_size("tile")
    blocks = jnp.concatenate([coords, fields], axis=1)
    prior = lax.ppermute(blocks, "tile", [(i, i + 1) for i in range(n_tile - 1)])
    table = lax.all_gather(jnp.stack([blocks, prior]), "wide", axis=0)
    smem = pl.BlockSpec(memory_space=pltpu.SMEM)
    vmem = pl.BlockSpec(memory_space=pltpu.VMEM)
    result, logs = pl.pallas_call(
        lambda *refs: whiten_kernel(n_wide, slots, *refs),
        out_shape=(
            jax.ShapeDtypeStruct((slots, 4, B), f32),
            jax.ShapeDtypeStruct((SUB, B), f32),
        ),
        in_specs=[smem, smem, smem, vmem, vmem, vmem],
        out_specs=(vmem, vmem),
        scratch_shapes=[
            pltpu.VMEM((NB, SUB * NB * B, B), f32),
            pltpu.VMEM((SUB * B, B), f32),
            pltpu.VMEM((B, B), f32),
            pltpu.VMEM((B, B), f32),
            pltpu.VMEM((NB, slots, SUB, B), f32),
            pltpu.VMEM((SUB * PANEL, B), f32),
        ],
        compiler_params=pltpu.CompilerParams(vmem_limit_bytes=48 << 20),
    )(counts, place, neighbours, coords, fields, table)
    return result, logs[:slots, 0]


def solution(mesh):
    in_specs = (
        P(("tile", "wide"), None, None),
        P(("tile", "wide"), None, None),
        P("tile", None),
        P(),
        P("tile", None),
    )
    out_specs = (P(("tile", "wide"), None, None), P(("tile", "wide")))
    return jax.shard_map(local, mesh=mesh, in_specs=in_specs, out_specs=out_specs, check_vma=False)
```

```python
import math

import jax
import jax.numpy as jnp
from jax import lax
from jax.experimental import pallas as pl
from jax.experimental.pallas import tpu as pltpu
from jax.sharding import PartitionSpec as P

B = 128
K = 3
NB = K + 1
SUB = 8
PANEL = 16
GROUP = 8

length_scale = 0.08
nugget = 0.25
root_three = math.sqrt(3.0)

f32 = jnp.float32
bf16 = jnp.bfloat16


def pieces(a):
    first = a.astype(bf16)
    rest = a - first.astype(f32)
    second = rest.astype(bf16)
    return first, second, (rest - second.astype(f32)).astype(bf16)


def left(a):
    first, second, third = pieces(a)
    return jnp.concatenate([first, second], axis=1), jnp.concatenate([first, third], axis=1)


def right_rows(b):
    first, second, third = pieces(b)
    main = jnp.concatenate(
        [jnp.concatenate([first, first], axis=1), jnp.concatenate([second, second], axis=1)], axis=0)
    return main, jnp.concatenate([third, first], axis=1)


def swap_sweep(panel, swept):
    a, b, c = pieces(panel)
    x, y, z = pieces(swept)
    return jnp.concatenate([a, a, b, b, a, c], axis=0).T, jnp.concatenate([x, y, x, y, z, x], axis=0)


def product(a, b):
    def dot(x, y):
        return lax.dot_general(x, y, (((1,), (1,)), ((), ())), preferred_element_type=f32)

    wide = dot(a[0], b[0])
    return wide[:, :B] + (wide[:, B:] + dot(a[1], b[1]))


def left_short(a):
    first = a.astype(bf16)
    return jnp.concatenate([first, (a - first.astype(f32)).astype(bf16)], axis=1)


def right_short(x):
    first = x[:, :B]
    return jnp.concatenate(
        [jnp.concatenate([first, first], axis=1),
         jnp.concatenate([x[:, B:], jnp.zeros_like(first)], axis=1)], axis=0)


def product_short(a, b):
    wide = lax.dot_general(a, b, (((1,), (1,)), ((), ())), preferred_element_type=f32)
    return wide[:, :B] + wide[:, B:]


def column(v, at):
    return jnp.broadcast_to(v[:, at : at + 1], v.shape)


def eliminate(rows, first, lane):
    n = len(rows)
    pivots = []
    scaled = []
    for g in range(0, n, GROUP):
        end = g + GROUP
        cols = {}
        for s in range(g, end):
            for i in range(s, n):
                cols[i, s] = column(rows[i], first + s)
        for t in range(g, end):
            pivot = cols[t, t]
            inv = 1.0 / pivot
            pivots.append(pivot)
            scaled.append(jnp.where(lane == first + t, 1.0 + pivot, rows[t]) * inv)
            for u in range(t + 1, end):
                lower = cols[u, t] * inv
                for i in range(u, n):
                    cols[i, u] = cols[i, u] - cols[i, t] * lower
                rows[u] = rows[u] - cols[u, t] * scaled[t]
            for i in range(end, n):
                rows[i] = rows[i] - cols[i, t] * scaled[t]
    return pivots, scaled


def whiten_kernel(
    n_wide, slots, counts_ref, place_ref, near_ref, coords_ref, fields_ref, table_ref,
    out_ref, logdet_ref, cov, weight, sites, sites_t, rhs, panel, swept,
):
    tile_index = lax.axis_index("tile")
    wide_index = lax.axis_index("wide")
    lane = lax.broadcasted_iota(jnp.int32, (SUB, B), 1)

    sites[...] = jnp.zeros_like(sites)
    rhs[...] = jnp.zeros_like(rhs)
    valid = {}
    for m in range(slots):
        for k in range(K):
            listed = near_ref[wide_index * slots + m, k]
            valid[m, k] = (listed >= 0).astype(f32)
            source = place_ref[jnp.maximum(listed, 0)]
            device = source // slots
            prior = (device // n_wide != tile_index).astype(jnp.int32)
            block = table_ref[device % n_wide, prior, source % slots]
            sites[pl.ds(m * SUB + k, 1), :] = block[0:1]
            sites[pl.ds(m * SUB + NB + k, 1), :] = block[1:2]
            rhs[k, m, 0:4, :] = block[2:6] * valid[m, k]
        sites[pl.ds(m * SUB + K, 1), :] = coords_ref[m, 0:1, :]
        sites[pl.ds(m * SUB + NB + K, 1), :] = coords_ref[m, 1:2, :]
        rhs[K, m, 0:4, :] = fields_ref[m]
        valid[m, K] = 1.0
    sites_t[...] = sites[...].T

    row_id = lax.broadcasted_iota(jnp.int32, (B, B), 0)
    col_id = lax.broadcasted_iota(jnp.int32, (B, B), 1)
    for m in range(slots):
        for c in range(NB):
            at = m * SUB + c
            x_row = jnp.broadcast_to(sites_t[:, at : at + 1], (B, B))
            y_row = jnp.broadcast_to(sites_t[:, at + NB : at + NB + 1], (B, B))
            for r in range(c + 1):
                dx = x_row - sites[pl.ds(m * SUB + r, 1), :]
                dy = y_row - sites[pl.ds(m * SUB + NB + r, 1), :]
                squared = dx * dx + dy * dy
                scaled = squared * (root_three / length_scale * lax.rsqrt(jnp.maximum(squared, 1e-30)))
                value = (1.0 + scaled) * jnp.exp(-scaled)
                if r < K:
                    value = value * (valid[m, c] * valid[m, r])
                if c == r:
                    value = value + jnp.where(row_id == col_id, nugget + 1.0 - valid[m, c], 0.0)
                cov[r, (m * NB + c) * B : (m * NB + c + 1) * B, :] = value

    def block_step(r, dets):
        mine = cov.at[r]
        start = pl.multiple_of(r * B, B)
        for p in range(0, B, PANEL):
            rows = [mine[pl.ds(start + p + t, SUB, stride=NB * B), :] for t in range(PANEL)]
            pivots, scaled = eliminate(rows, p, lane)
            for t in range(PANEL):
                own = jnp.where(lane < p + t, rows[t], jnp.where(lane == p + t, 1.0, 0.0))
                weight[pl.ds(p + t, SUB, stride=B), :] = own * lax.rsqrt(pivots[t])
                dets = jnp.where(lane == p + t, pivots[t], dets)
                panel[pl.ds(t, SUB, stride=PANEL), :] = rows[t]
                swept[pl.ds(t, SUB, stride=PANEL), :] = scaled[t]
            rest = B - p - PANEL
            if rest == 0:
                continue
            for m in range(slots):
                base = start + m * NB * B
                these = slice(m * PANEL, (m + 1) * PANEL)
                turned, sweep = swap_sweep(panel[these, :], swept[these, :])
                change = lax.dot_general(
                    turned[p + PANEL :], sweep, (((1,), (0,)), ((), ())), preferred_element_type=f32)
                here = pl.ds(base + p + PANEL, rest)
                mine[here, :] = mine[here, :] - change

        for at in range(NB):
            pl.when(r == at)(lambda at=at: couple(at))
        return dets

    def couple(r):
        later = (NB - 1 - r) * B
        for m in range(slots):
            w = right_rows(weight[m * B : (m + 1) * B, :])
            rhs[r, m] = product(left(rhs[r, m]), w)
            if r < K:
                there = pl.ds((m * NB + r + 1) * B, later)
                cov[r, there, :] = product(left(cov[r, there, :]), w)
        for m in range(slots if r < K else 0):
            x = left_short(cov[r, pl.ds((m * NB + r + 1) * B, later), :])
            z = left_short(rhs[r, m])
            for e in range(r + 1, NB):
                skip = (e - r - 1) * B
                y = right_short(x[skip : skip + B])
                here = pl.ds((m * NB + e) * B, later - skip)
                cov[e, here, :] = cov[e, here, :] - product_short(x[skip:], y)
                rhs[e, m] = rhs[e, m] - product_short(z, y)

    dets = lax.fori_loop(0, NB, block_step, jnp.ones((SUB, B), f32))
    total = jnp.sum(jnp.log(dets), axis=1, keepdims=True)
    live_count = counts_ref[0, wide_index]
    slot_id = lax.broadcasted_iota(jnp.int32, (SUB, 1), 0)
    logdet_ref[...] = jnp.broadcast_to(jnp.where(slot_id < live_count, total, 0.0), (SUB, B))
    for m in range(slots):
        live = (m < live_count).astype(f32)
        out_ref[m] = rhs[K, m, 0:4, :] * live


def local(coords, fields, counts, place, neighbours):
    slots = coords.shape[0]
    n_wide = lax.axis_size("wide")
    n_tile = lax.axis_size("tile")
    blocks = jnp.concatenate([coords, fields], axis=1)
    prior = lax.ppermute(blocks, "tile", [(i, i + 1) for i in range(n_tile - 1)])
    table = lax.all_gather(jnp.stack([blocks, prior]), "wide", axis=0)
    smem = pl.BlockSpec(memory_space=pltpu.SMEM)
    vmem = pl.BlockSpec(memory_space=pltpu.VMEM)
    result, logs = pl.pallas_call(
        lambda *refs: whiten_kernel(n_wide, slots, *refs),
        out_shape=(
            jax.ShapeDtypeStruct((slots, 4, B), f32),
            jax.ShapeDtypeStruct((SUB, B), f32),
        ),
        in_specs=[smem, smem, smem, vmem, vmem, vmem],
        out_specs=(vmem, vmem),
        scratch_shapes=[
            pltpu.VMEM((NB, SUB * NB * B, B), f32),
            pltpu.VMEM((SUB * B, B), f32),
            pltpu.VMEM((B, B), f32),
            pltpu.VMEM((B, B), f32),
            pltpu.VMEM((NB, slots, SUB, B), f32),
            pltpu.VMEM((SUB * PANEL, B), f32),
            pltpu.VMEM((SUB * PANEL, B), f32),
        ],
        compiler_params=pltpu.CompilerParams(vmem_limit_bytes=48 << 20),
    )(counts, place, neighbours, coords, fields, table)
    return result, logs[:slots, 0]


def solution(mesh):
    in_specs = (
        P(("tile", "wide"), None, None),
        P(("tile", "wide"), None, None),
        P("tile", None),
        P(),
        P("tile", None),
    )
    out_specs = (P(("tile", "wide"), None, None), P(("tile", "wide")))
    return jax.shard_map(local, mesh=mesh, in_specs=in_specs, out_specs=out_specs, check_vma=False)
```

```python
import math

import jax
import jax.numpy as jnp
from jax import lax
from jax.experimental import pallas as pl
from jax.experimental.pallas import tpu as pltpu
from jax.sharding import PartitionSpec as P

B = 128
K = 3
NB = K + 1
SUB = 8
PANEL = 16
GROUP = 8
LOOK = 1
TAIL = 1
DEFER = True

length_scale = 0.08
nugget = 0.25
root_three = math.sqrt(3.0)

f32 = jnp.float32
bf16 = jnp.bfloat16


def pieces(a):
    first = a.astype(bf16)
    rest = a - first.astype(f32)
    second = rest.astype(bf16)
    return first, second, (rest - second.astype(f32)).astype(bf16)


def left(a):
    first, second, third = pieces(a)
    return jnp.concatenate([first, second], axis=1), jnp.concatenate([first, third], axis=1)


def right_rows(b):
    first, second, third = pieces(b)
    main = jnp.concatenate(
        [jnp.concatenate([first, first], axis=1), jnp.concatenate([second, second], axis=1)], axis=0)
    return main, jnp.concatenate([third, first], axis=1)


def swap_sweep(panel, swept):
    a, b, c = pieces(panel)
    x, y, z = pieces(swept)
    return jnp.concatenate([a, a, b, b, a, c], axis=0).T, jnp.concatenate([x, y, x, y, z, x], axis=0)


def product(a, b):
    def dot(x, y):
        return lax.dot_general(x, y, (((1,), (1,)), ((), ())), preferred_element_type=f32)

    wide = dot(a[0], b[0])
    return wide[:, :B] + (wide[:, B:] + dot(a[1], b[1]))


def left_short(a):
    first = a.astype(bf16)
    return jnp.concatenate([first, (a - first.astype(f32)).astype(bf16)], axis=1)


def right_short(x):
    first = x[:, :B]
    return jnp.concatenate(
        [jnp.concatenate([first, first], axis=1),
         jnp.concatenate([x[:, B:], jnp.zeros_like(first)], axis=1)], axis=0)


def product_short(a, b):
    wide = lax.dot_general(a, b, (((1,), (1,)), ((), ())), preferred_element_type=f32)
    return wide[:, :B] + wide[:, B:]


def column(v, at):
    return jnp.broadcast_to(v[:, at : at + 1], v.shape)


def eliminate(rows, first, lane):
    n = len(rows)
    pivots = []
    scaled = []
    for g in range(0, n, GROUP):
        end = g + GROUP
        cols = {}
        for s in range(g, end):
            for i in range(s, n):
                cols[i, s] = column(rows[i], first + s)
        for t in range(g, end):
            pivot = cols[t, t]
            inv = 1.0 / pivot
            pivots.append(pivot)
            scaled.append(jnp.where(lane == first + t, 1.0 + pivot, rows[t]) * inv)
            for u in range(t + 1, end):
                lower = cols[u, t] * inv
                for i in range(u, n):
                    cols[i, u] = cols[i, u] - cols[i, t] * lower
                rows[u] = rows[u] - cols[u, t] * scaled[t]
            for i in range(end, n):
                rows[i] = rows[i] - cols[i, t] * scaled[t]
    return pivots, scaled


def whiten_kernel(
    n_wide, slots, counts_ref, place_ref, near_ref, coords_ref, fields_ref, table_ref,
    out_ref, logdet_ref, cov, weight, sites, sites_t, rhs, panel, swept,
):
    tile_index = lax.axis_index("tile")
    wide_index = lax.axis_index("wide")
    lane = lax.broadcasted_iota(jnp.int32, (SUB, B), 1)

    sites[...] = jnp.zeros_like(sites)
    rhs[...] = jnp.zeros_like(rhs)
    valid = {}
    for m in range(slots):
        for k in range(K):
            listed = near_ref[wide_index * slots + m, k]
            valid[m, k] = (listed >= 0).astype(f32)
            source = place_ref[jnp.maximum(listed, 0)]
            device = source // slots
            prior = (device // n_wide != tile_index).astype(jnp.int32)
            block = table_ref[device % n_wide, prior, source % slots]
            sites[pl.ds(m * SUB + k, 1), :] = block[0:1]
            sites[pl.ds(m * SUB + NB + k, 1), :] = block[1:2]
            rhs[k, m, 0:4, :] = block[2:6] * valid[m, k]
        sites[pl.ds(m * SUB + K, 1), :] = coords_ref[m, 0:1, :]
        sites[pl.ds(m * SUB + NB + K, 1), :] = coords_ref[m, 1:2, :]
        rhs[K, m, 0:4, :] = fields_ref[m]
        valid[m, K] = 1.0
    sites_t[...] = sites[...].T

    row_id = lax.broadcasted_iota(jnp.int32, (B, B), 0)
    col_id = lax.broadcasted_iota(jnp.int32, (B, B), 1)

    def covariance(m, c, columns):
        at = m * SUB + c
        x_row = jnp.broadcast_to(sites_t[:, at : at + 1], (B, B))
        y_row = jnp.broadcast_to(sites_t[:, at + NB : at + NB + 1], (B, B))
        for r in columns:
            dx = x_row - sites[pl.ds(m * SUB + r, 1), :]
            dy = y_row - sites[pl.ds(m * SUB + NB + r, 1), :]
            squared = dx * dx + dy * dy
            scaled = squared * (root_three / length_scale * lax.rsqrt(jnp.maximum(squared, 1e-30)))
            value = (1.0 + scaled) * jnp.exp(-scaled)
            if r < K:
                value = value * (valid[m, c] * valid[m, r])
            if c == r:
                value = value + jnp.where(row_id == col_id, nugget + 1.0 - valid[m, c], 0.0)
            cov[r, (m * NB + c) * B : (m * NB + c + 1) * B, :] = value

    for m in range(slots):
        covariance(m, 0, (0,))
    later_work = [
        lambda m=m, c=c: covariance(m, c, range(c + 1)) for c in range(1, NB) for m in range(slots)]

    def factor_block(r):
        mine = cov.at[r]
        rest_of_panel = []
        pivot_rows = []
        for p in range(0, B, PANEL):
            rows = [mine[pl.ds(r * B + p + t, SUB, stride=NB * B), :] for t in range(PANEL)]
            pivots, scaled = eliminate(rows, p, lane)
            pivot_rows += pivots
            for work in rest_of_panel:
                work()
            rest_of_panel.clear()
            for t in range(PANEL):
                panel[pl.ds(t, SUB, stride=PANEL), :] = rows[t]
                swept[pl.ds(t, SUB, stride=PANEL), :] = scaled[t]
            start = p + PANEL
            if start < B:
                turns = []
                for m in range(slots):
                    these = slice(m * PANEL, (m + 1) * PANEL)
                    turned, sweep = swap_sweep(panel[these, :], swept[these, :])
                    turns.append((turned, sweep))

                def update(m, first, last, turned, sweep):
                    here = pl.ds((m * NB + r) * B + first, last - first)
                    mine[here, :] = mine[here, :] - lax.dot_general(
                        turned[first:last], sweep, (((1,), (0,)), ((), ())), preferred_element_type=f32)

                soon = min(B, start + LOOK * PANEL)
                for m in range(slots):
                    update(m, start, soon, *turns[m])
                if soon < B:
                    rest_of_panel += [
                        lambda m=m, a=soon, t=turns[m]: update(m, a, B, *t) for m in range(slots)]
            for t in range(PANEL):
                own = jnp.where(lane < p + t, rows[t], jnp.where(lane == p + t, 1.0, 0.0))
                weight[r % 2, pl.ds(p + t, SUB, stride=B), :] = own * lax.rsqrt(pivots[t])
            for _ in range(-(-len(later_work) // max(1, (B - p) // PANEL - TAIL))):
                later_work.pop(0)()
        return pivot_rows

    def solve(r, m, c, count):
        w = right_rows(weight[r % 2, m * B : (m + 1) * B, :])
        there = pl.ds((m * NB + c) * B, count * B)
        cov[r, there, :] = product(left(cov[r, there, :]), w)

    def update_block(r, m, c, count, e):
        x = left_short(cov[r, pl.ds((m * NB + c) * B, count * B), :])
        y = right_short(left_short(cov[r, pl.ds((m * NB + e) * B, B), :]))
        here = pl.ds((m * NB + c) * B, count * B)
        cov[e, here, :] = cov[e, here, :] - product_short(x, y)

    def finish_rhs(r, m):
        w = right_rows(weight[r % 2, m * B : (m + 1) * B, :])
        solved = product(left(rhs[r, m]), w)
        rhs[r, m] = solved
        z = left_short(solved)
        for e in range(r + 1, NB):
            y = right_short(left_short(cov[r, pl.ds((m * NB + e) * B, B), :]))
            rhs[e, m] = rhs[e, m] - product_short(z, y)

    def rest_of_block(r, m):
        if r + 2 < NB:
            solve(r, m, r + 2, NB - r - 2)
            update_block(r, m, r + 2, NB - r - 2, r + 1)
            for e in range(r + 2, NB):
                update_block(r, m, e, NB - e, e)
        finish_rhs(r, m)

    for r in range(NB):
        pivot_rows = factor_block(r)
        if r < K:
            for m in range(slots):
                solve(r, m, r + 1, 1)
            for m in range(slots):
                update_block(r, m, r + 1, 1, r + 1)
        later_work += [lambda r=r, m=m: rest_of_block(r, m) for m in range(slots)]
        if not DEFER or r == K:
            for work in later_work:
                work()
            later_work.clear()
    dets = pivot_rows[0]
    for t in range(1, B):
        dets = jnp.where(lane == t, pivot_rows[t], dets)
    total = jnp.sum(jnp.log(dets), axis=1, keepdims=True)
    live_count = counts_ref[0, wide_index]
    for m in range(slots):
        logdet_ref[m] = jnp.where(m < live_count, total[m, 0], 0.0)
    for m in range(slots):
        live = (m < live_count).astype(f32)
        out_ref[m] = rhs[K, m, 0:4, :] * live


def local(coords, fields, counts, place, neighbours):
    slots = coords.shape[0]
    n_wide = lax.axis_size("wide")
    n_tile = lax.axis_size("tile")
    blocks = jnp.concatenate([coords, fields], axis=1)
    prior = lax.ppermute(blocks, "tile", [(i, i + 1) for i in range(n_tile - 1)])
    table = lax.all_gather(jnp.stack([blocks, prior]), "wide", axis=0)
    smem = pl.BlockSpec(memory_space=pltpu.SMEM)
    vmem = pl.BlockSpec(memory_space=pltpu.VMEM)
    return pl.pallas_call(
        lambda *refs: whiten_kernel(n_wide, slots, *refs),
        out_shape=(
            jax.ShapeDtypeStruct((slots, 4, B), f32),
            jax.ShapeDtypeStruct((slots,), f32),
        ),
        in_specs=[smem, smem, smem, vmem, vmem, vmem],
        out_specs=(vmem, smem),
        scratch_shapes=[
            pltpu.VMEM((NB, SUB * NB * B, B), f32),
            pltpu.VMEM((2, SUB * B, B), f32),
            pltpu.VMEM((B, B), f32),
            pltpu.VMEM((B, B), f32),
            pltpu.VMEM((NB, slots, SUB, B), f32),
            pltpu.VMEM((SUB * PANEL, B), f32),
            pltpu.VMEM((SUB * PANEL, B), f32),
        ],
        compiler_params=pltpu.CompilerParams(vmem_limit_bytes=48 << 20),
    )(counts, place, neighbours, coords, fields, table)


def solution(mesh):
    in_specs = (
        P(("tile", "wide"), None, None),
        P(("tile", "wide"), None, None),
        P("tile", None),
        P(),
        P("tile", None),
    )
    out_specs = (P(("tile", "wide"), None, None), P(("tile", "wide")))
    return jax.shard_map(local, mesh=mesh, in_specs=in_specs, out_specs=out_specs, check_vma=False)
```

```python
import math

import jax
import jax.numpy as jnp
from jax import lax
from jax.experimental import pallas as pl
from jax.experimental.pallas import tpu as pltpu
from jax.sharding import PartitionSpec as P

B = 128
K = 3
NB = K + 1
SUB = 8
PANEL = 16
GROUP = 8
COV = NB * B + 8
FACTOR = B + 8
SWEEP = PANEL + 8
LOOK = 1
TAIL = 1
DEFER = True

length_scale = 0.08
nugget = 0.25
root_three = math.sqrt(3.0)

f32 = jnp.float32
bf16 = jnp.bfloat16


def pieces(a):
    first = a.astype(bf16)
    rest = a - first.astype(f32)
    second = rest.astype(bf16)
    return first, second, (rest - second.astype(f32)).astype(bf16)


def left(a):
    first, second, third = pieces(a)
    return jnp.concatenate([first, second], axis=1), jnp.concatenate([first, third], axis=1)


def right_rows(b):
    first, second, third = pieces(b)
    main = jnp.concatenate(
        [jnp.concatenate([first, first], axis=1), jnp.concatenate([second, second], axis=1)], axis=0)
    return main, jnp.concatenate([third, first], axis=1)


def swap_sweep(panel, swept):
    a, b, c = pieces(panel)
    x, y, z = pieces(swept)
    return jnp.concatenate([a, a, b, b, a, c], axis=0).T, jnp.concatenate([x, y, x, y, z, x], axis=0)


def product(a, b):
    def dot(x, y):
        return lax.dot_general(x, y, (((1,), (1,)), ((), ())), preferred_element_type=f32)

    wide = dot(a[0], b[0])
    return wide[:, :B] + (wide[:, B:] + dot(a[1], b[1]))


def left_short(a):
    first = a.astype(bf16)
    return jnp.concatenate([first, (a - first.astype(f32)).astype(bf16)], axis=1)


def right_short(x):
    first = x[:, :B]
    return jnp.concatenate(
        [jnp.concatenate([first, first], axis=1),
         jnp.concatenate([x[:, B:], jnp.zeros_like(first)], axis=1)], axis=0)


def product_short(a, b):
    wide = lax.dot_general(a, b, (((1,), (1,)), ((), ())), preferred_element_type=f32)
    return wide[:, :B] + wide[:, B:]


def column(v, at):
    return jnp.broadcast_to(v[:, at : at + 1], v.shape)


def eliminate(rows, first, lane):
    n = len(rows)
    pivots = []
    scaled = []
    for g in range(0, n, GROUP):
        end = g + GROUP
        cols = {}
        for s in range(g, end):
            for i in range(s, n):
                cols[i, s] = column(rows[i], first + s)
        for t in range(g, end, 2):
            v = t + 1
            pivot = cols[t, t]
            cross = cols[v, t]
            inv = 1.0 / pivot
            both = pivot * cols[v, v] - cross * cross
            inv_next = pivot * (1.0 / both)
            lower = cross * inv
            next_pivot = cols[v, v] - cross * lower
            pivots += [pivot, next_pivot]
            head = jnp.where(lane == first + t, 1.0 + pivot, rows[t]) * inv
            rows[v] = rows[v] - cross * head
            tail = jnp.where(lane == first + v, 1.0 + next_pivot, rows[v]) * inv_next
            scaled += [head, tail]
            after = {i: cols[i, v] - cols[i, t] * lower for i in range(v + 1, n)}
            for u in range(v + 1, end):
                one = cols[u, t] * inv
                two = after[u] * inv_next
                for i in range(u, n):
                    cols[i, u] = cols[i, u] - cols[i, t] * one - after[i] * two
            for i in range(v + 1, n):
                rows[i] = rows[i] - cols[i, t] * head - after[i] * tail
    return pivots, scaled


def whiten_kernel(
    n_wide, slots, n_place, meta_ref, table_ref,
    out_ref, logdet_ref, cov, weight, sites, sites_t, rhs, panel, swept,
):
    tile_index = lax.axis_index("tile")
    wide_index = lax.axis_index("wide")
    lane = lax.broadcasted_iota(jnp.int32, (SUB, B), 1)

    sites[...] = jnp.zeros_like(sites)
    rhs[...] = jnp.zeros_like(rhs)
    valid = {}
    for m in range(slots):
        for k in range(K):
            listed = meta_ref[n_wide + n_place + (wide_index * slots + m) * K + k]
            valid[m, k] = (listed >= 0).astype(f32)
            source = meta_ref[n_wide + jnp.maximum(listed, 0)]
            device = source // slots
            tile = device // n_wide
            prior = (tile != tile_index).astype(jnp.int32)
            block = table_ref[device - tile * n_wide, prior, source - device * slots]
            sites[pl.ds(m * SUB + k, 1), :] = block[0:1]
            sites[pl.ds(m * SUB + NB + k, 1), :] = block[1:2]
            rhs[k, m, 0:4, :] = block[2:6] * valid[m, k]
        block = table_ref[wide_index, 0, m]
        sites[pl.ds(m * SUB + K, 1), :] = block[0:1]
        sites[pl.ds(m * SUB + NB + K, 1), :] = block[1:2]
        rhs[K, m, 0:4, :] = block[2:6]
        valid[m, K] = 1.0
    sites_t[...] = sites[...].T

    row_id = lax.broadcasted_iota(jnp.int32, (B, B), 0)
    col_id = lax.broadcasted_iota(jnp.int32, (B, B), 1)

    def covariance(m, c, columns):
        at = m * SUB + c
        x_row = jnp.broadcast_to(sites_t[:, at : at + 1], (B, B))
        y_row = jnp.broadcast_to(sites_t[:, at + NB : at + NB + 1], (B, B))
        for r in columns:
            dx = x_row - sites[pl.ds(m * SUB + r, 1), :]
            dy = y_row - sites[pl.ds(m * SUB + NB + r, 1), :]
            squared = dx * dx + dy * dy
            scaled = squared * (root_three / length_scale * lax.rsqrt(jnp.maximum(squared, 1e-30)))
            value = (1.0 + scaled) * jnp.exp(-scaled)
            if r < K:
                value = value * (valid[m, c] * valid[m, r])
            if c == r:
                value = value + jnp.where(row_id == col_id, nugget + 1.0 - valid[m, c], 0.0)
            cov[r, m * COV + c * B : m * COV + (c + 1) * B, :] = value

    for m in range(slots):
        covariance(m, 0, (0,))
    later_work = [
        lambda m=m, c=c: covariance(m, c, range(c + 1)) for c in range(1, NB) for m in range(slots)]

    def factor_block(r):
        mine = cov.at[r]
        rest_of_panel = []
        pivot_rows = []
        for p in range(0, B, PANEL):
            rows = [mine[pl.ds(r * B + p + t, SUB, stride=COV), :] for t in range(PANEL)]
            pivots, scaled = eliminate(rows, p, lane)
            pivot_rows += pivots
            for work in rest_of_panel:
                work()
            rest_of_panel.clear()
            for t in range(PANEL):
                panel[pl.ds(t, SUB, stride=SWEEP), :] = rows[t]
                swept[pl.ds(t, SUB, stride=SWEEP), :] = scaled[t]
            start = p + PANEL
            if start < B:
                turns = []
                for m in range(slots):
                    these = slice(m * SWEEP, m * SWEEP + PANEL)
                    turned, sweep = swap_sweep(panel[these, :], swept[these, :])
                    turns.append((turned, sweep))

                def update(m, first, last, turned, sweep):
                    here = pl.ds(m * COV + r * B + first, last - first)
                    mine[here, :] = mine[here, :] - lax.dot_general(
                        turned[first:last], sweep, (((1,), (0,)), ((), ())), preferred_element_type=f32)

                soon = min(B, start + LOOK * PANEL)
                for m in range(slots):
                    update(m, start, soon, *turns[m])
                if soon < B:
                    rest_of_panel += [
                        lambda m=m, a=soon, t=turns[m]: update(m, a, B, *t) for m in range(slots)]
            for t in range(PANEL):
                own = jnp.where(lane < p + t, rows[t], jnp.where(lane == p + t, 1.0, 0.0))
                weight[r % 2, pl.ds(p + t, SUB, stride=FACTOR), :] = own * lax.rsqrt(pivots[t])
            for _ in range(-(-len(later_work) // max(1, (B - p) // PANEL - TAIL))):
                later_work.pop(0)()
        return pivot_rows

    def solve(r, m, c, count):
        w = right_rows(weight[r % 2, m * FACTOR : m * FACTOR + B, :])
        there = pl.ds(m * COV + c * B, count * B)
        cov[r, there, :] = product(left(cov[r, there, :]), w)

    def update_block(r, m, c, count, e):
        x = left_short(cov[r, pl.ds(m * COV + c * B, count * B), :])
        y = right_short(left_short(cov[r, pl.ds(m * COV + e * B, B), :]))
        here = pl.ds(m * COV + c * B, count * B)
        cov[e, here, :] = cov[e, here, :] - product_short(x, y)

    def finish_rhs(r, m):
        w = right_rows(weight[r % 2, m * FACTOR : m * FACTOR + B, :])
        solved = product(left(rhs[r, m]), w)
        rhs[r, m] = solved
        z = left_short(solved)
        for e in range(r + 1, NB):
            y = right_short(left_short(cov[r, pl.ds(m * COV + e * B, B), :]))
            rhs[e, m] = rhs[e, m] - product_short(z, y)

    def rest_of_block(r, m):
        if r + 2 < NB:
            solve(r, m, r + 2, NB - r - 2)
            update_block(r, m, r + 2, NB - r - 2, r + 1)
            for e in range(r + 2, NB):
                update_block(r, m, e, NB - e, e)
        finish_rhs(r, m)

    for r in range(NB):
        pivot_rows = factor_block(r)
        if r < K:
            for m in range(slots):
                solve(r, m, r + 1, 1)
            for m in range(slots):
                update_block(r, m, r + 1, 1, r + 1)
        later_work += [lambda r=r, m=m: rest_of_block(r, m) for m in range(slots)]
        if not DEFER or r == K:
            for work in later_work:
                work()
            later_work.clear()
    dets = pivot_rows[0]
    for t in range(1, B):
        dets = jnp.where(lane == t, pivot_rows[t], dets)
    total = jnp.sum(jnp.log(dets), axis=1, keepdims=True)
    live_count = meta_ref[wide_index]
    for m in range(slots):
        logdet_ref[m] = jnp.where(m < live_count, total[m, 0], 0.0)
    for m in range(slots):
        live = (m < live_count).astype(f32)
        out_ref[m] = rhs[K, m, 0:4, :] * live


def local(coords, fields, counts, place, neighbours):
    slots = coords.shape[0]
    n_wide = lax.axis_size("wide")
    n_tile = lax.axis_size("tile")
    blocks = jnp.concatenate([coords, fields], axis=1)
    prior = lax.ppermute(blocks, "tile", [(i, i + 1) for i in range(n_tile - 1)])
    table = lax.all_gather(jnp.stack([blocks, prior]), "wide", axis=0)
    meta = jnp.concatenate([counts.reshape(-1), place, neighbours.reshape(-1)])
    smem = pl.BlockSpec(memory_space=pltpu.SMEM)
    vmem = pl.BlockSpec(memory_space=pltpu.VMEM)
    return pl.pallas_call(
        lambda *refs: whiten_kernel(n_wide, slots, place.shape[0], *refs),
        out_shape=(
            jax.ShapeDtypeStruct((slots, 4, B), f32),
            jax.ShapeDtypeStruct((slots,), f32),
        ),
        in_specs=[smem, vmem],
        out_specs=(vmem, smem),
        scratch_shapes=[
            pltpu.VMEM((NB, (SUB + 1) * COV, B), f32),
            pltpu.VMEM((2, (SUB + 1) * FACTOR, B), f32),
            pltpu.VMEM((B, B), f32),
            pltpu.VMEM((B, B), f32),
            pltpu.VMEM((NB, slots, SUB, B), f32),
            pltpu.VMEM(((SUB + 1) * SWEEP, B), f32),
            pltpu.VMEM(((SUB + 1) * SWEEP, B), f32),
        ],
        compiler_params=pltpu.CompilerParams(vmem_limit_bytes=48 << 20),
    )(meta, table)


def solution(mesh):
    in_specs = (
        P(("tile", "wide"), None, None),
        P(("tile", "wide"), None, None),
        P("tile", None),
        P(),
        P("tile", None),
    )
    out_specs = (P(("tile", "wide"), None, None), P(("tile", "wide")))
    return jax.shard_map(local, mesh=mesh, in_specs=in_specs, out_specs=out_specs, check_vma=False)
```

```python
import math

import jax
import jax.numpy as jnp
from jax import lax
from jax.experimental import pallas as pl
from jax.experimental.pallas import tpu as pltpu
from jax.sharding import PartitionSpec as P

B = 128
K = 3
NB = K + 1
SUB = 8
PANEL = 16
GROUP = 8
COV = NB * B + 8
FACTOR = B + 8
SWEEP = PANEL + 8
LOOK = 1
TAIL = 1
DEFER = True

length_scale = 0.08
nugget = 0.25
root_three = math.sqrt(3.0)

f32 = jnp.float32
bf16 = jnp.bfloat16


def pieces(a):
    first = a.astype(bf16)
    rest = a - first.astype(f32)
    second = rest.astype(bf16)
    return first, second, (rest - second.astype(f32)).astype(bf16)


def left(a):
    first, second, third = pieces(a)
    return jnp.concatenate([first, second], axis=1), jnp.concatenate([first, third], axis=1)


def right_rows(b):
    first, second, third = pieces(b)
    main = jnp.concatenate(
        [jnp.concatenate([first, first], axis=1), jnp.concatenate([second, second], axis=1)], axis=0)
    return main, jnp.concatenate([third, first], axis=1)


def swap_sweep(panel, swept):
    a, b, c = pieces(panel)
    x, y, z = pieces(swept)
    return jnp.concatenate([a, a, b, b, a, c], axis=0).T, jnp.concatenate([x, y, x, y, z, x], axis=0)


def product(a, b):
    def dot(x, y):
        return lax.dot_general(x, y, (((1,), (1,)), ((), ())), preferred_element_type=f32)

    wide = dot(a[0], b[0])
    return wide[:, :B] + (wide[:, B:] + dot(a[1], b[1]))


def left_short(a):
    first = a.astype(bf16)
    return jnp.concatenate([first, (a - first.astype(f32)).astype(bf16)], axis=1)


def right_short(x):
    first = x[:, :B]
    return jnp.concatenate(
        [jnp.concatenate([first, first], axis=1),
         jnp.concatenate([x[:, B:], jnp.zeros_like(first)], axis=1)], axis=0)


def product_short(a, b):
    wide = lax.dot_general(a, b, (((1,), (1,)), ((), ())), preferred_element_type=f32)
    return wide[:, :B] + wide[:, B:]


def column(v, at):
    return jnp.broadcast_to(v[:, at : at + 1], v.shape)


def eliminate(rows, first, lane):
    n = len(rows)
    pivots = []
    scaled = []
    for g in range(0, n, GROUP):
        end = g + GROUP
        cols = {}
        for s in range(g, end):
            for i in range(s, n):
                cols[i, s] = column(rows[i], first + s)
        for t in range(g, end, 2):
            v = t + 1
            pivot = cols[t, t]
            cross = cols[v, t]
            inv = 1.0 / pivot
            both = pivot * cols[v, v] - cross * cross
            inv_next = pivot * (1.0 / both)
            lower = cross * inv
            next_pivot = cols[v, v] - cross * lower
            pivots += [pivot, next_pivot]
            head = jnp.where(lane == first + t, 1.0 + pivot, rows[t]) * inv
            rows[v] = rows[v] - cross * head
            tail = jnp.where(lane == first + v, 1.0 + next_pivot, rows[v]) * inv_next
            scaled += [head, tail]
            after = {i: cols[i, v] - cols[i, t] * lower for i in range(v + 1, n)}
            for u in range(v + 1, end):
                one = cols[u, t] * inv
                two = after[u] * inv_next
                for i in range(u, n):
                    cols[i, u] = cols[i, u] - cols[i, t] * one - after[i] * two
            for i in range(v + 1, n):
                rows[i] = rows[i] - cols[i, t] * head - after[i] * tail
    return pivots, scaled


def whiten_kernel(
    n_wide, slots, n_place, meta_ref, table_ref,
    out_ref, logdet_ref, cov, weight, sites, sites_t, rhs, panel, swept,
):
    tile_index = lax.axis_index("tile")
    wide_index = lax.axis_index("wide")
    lane = lax.broadcasted_iota(jnp.int32, (SUB, B), 1)

    sites[...] = jnp.zeros_like(sites)
    rhs[...] = jnp.zeros_like(rhs)
    valid = {}
    for m in range(slots):
        for k in range(K):
            listed = meta_ref[n_wide + n_place + (wide_index * slots + m) * K + k]
            valid[m, k] = (listed >= 0).astype(f32)
            source = meta_ref[n_wide + jnp.maximum(listed, 0)]
            device = source // slots
            tile = device // n_wide
            prior = (tile != tile_index).astype(jnp.int32)
            block = table_ref[device - tile * n_wide, prior, source - device * slots]
            sites[pl.ds(m * SUB + k, 1), :] = block[0:1]
            sites[pl.ds(m * SUB + NB + k, 1), :] = block[1:2]
            rhs[k, m, 0:4, :] = block[2:6] * valid[m, k]
        block = table_ref[wide_index, 0, m]
        sites[pl.ds(m * SUB + K, 1), :] = block[0:1]
        sites[pl.ds(m * SUB + NB + K, 1), :] = block[1:2]
        rhs[K, m, 0:4, :] = block[2:6]
        valid[m, K] = 1.0
    sites_t[...] = sites[...].T

    row_id = lax.broadcasted_iota(jnp.int32, (B, B), 0)
    col_id = lax.broadcasted_iota(jnp.int32, (B, B), 1)

    def covariance(m, c, columns):
        at = m * SUB + c
        x_row = jnp.broadcast_to(sites_t[:, at : at + 1], (B, B))
        y_row = jnp.broadcast_to(sites_t[:, at + NB : at + NB + 1], (B, B))
        for r in columns:
            dx = x_row - sites[pl.ds(m * SUB + r, 1), :]
            dy = y_row - sites[pl.ds(m * SUB + NB + r, 1), :]
            squared = dx * dx + dy * dy
            scaled = squared * (root_three / length_scale * lax.rsqrt(jnp.maximum(squared, 1e-30)))
            value = (1.0 + scaled) * jnp.exp(-scaled)
            if r < K:
                value = value * (valid[m, c] * valid[m, r])
            if c == r:
                value = value + jnp.where(row_id == col_id, nugget + 1.0 - valid[m, c], 0.0)
            cov[r, m * COV + c * B : m * COV + (c + 1) * B, :] = value

    for m in range(slots):
        covariance(m, 0, (0,))
    later_work = [
        lambda m=m, c=c: covariance(m, c, range(c + 1)) for c in range(1, NB) for m in range(slots)]

    def factor_block(r):
        mine = cov.at[r]
        rest_of_panel = []
        pivot_rows = []
        for p in range(0, B, PANEL):
            rows = [mine[pl.ds(r * B + p + t, SUB, stride=COV), :] for t in range(PANEL)]
            pivots, scaled = eliminate(rows, p, lane)
            pivot_rows += pivots
            for work in rest_of_panel:
                work()
            rest_of_panel.clear()
            for t in range(PANEL):
                panel[pl.ds(t, SUB, stride=SWEEP), :] = rows[t]
                swept[pl.ds(t, SUB, stride=SWEEP), :] = scaled[t]
            start = p + PANEL
            if start < B:
                turns = []
                for m in range(slots):
                    these = slice(m * SWEEP, m * SWEEP + PANEL)
                    turned, sweep = swap_sweep(panel[these, :], swept[these, :])
                    turns.append((turned, sweep))

                def update(m, first, last, turned, sweep):
                    here = pl.ds(m * COV + r * B + first, last - first)
                    mine[here, :] = mine[here, :] - lax.dot_general(
                        turned[first:last], sweep, (((1,), (0,)), ((), ())), preferred_element_type=f32)

                soon = min(B, start + LOOK * PANEL)
                for m in range(slots):
                    update(m, start, soon, *turns[m])
                if soon < B:
                    rest_of_panel += [
                        lambda m=m, a=soon, t=turns[m]: update(m, a, B, *t) for m in range(slots)]
            for t in range(PANEL):
                own = jnp.where(lane < p + t, rows[t], jnp.where(lane == p + t, 1.0, 0.0))
                weight[r % 2, pl.ds(p + t, SUB, stride=FACTOR), :] = own * lax.rsqrt(pivots[t])
            for _ in range(-(-len(later_work) // max(1, (B - p) // PANEL - TAIL))):
                later_work.pop(0)()
        return pivot_rows

    def solve(r, m, c, count):
        w = right_rows(weight[r % 2, m * FACTOR : m * FACTOR + B, :])
        there = pl.ds(m * COV + c * B, count * B)
        x = product(left(cov[r, there, :]), w)
        cov[r, there, :] = x
        return x

    def update_block(r, m, c, count, e):
        x = left_short(cov[r, pl.ds(m * COV + c * B, count * B), :])
        y = right_short(left_short(cov[r, pl.ds(m * COV + e * B, B), :]))
        here = pl.ds(m * COV + c * B, count * B)
        cov[e, here, :] = cov[e, here, :] - product_short(x, y)

    def finish_rhs(r, m):
        w = right_rows(weight[r % 2, m * FACTOR : m * FACTOR + B, :])
        solved = product(left(rhs[r, m]), w)
        rhs[r, m] = solved
        z = left_short(solved)
        for e in range(r + 1, NB):
            y = right_short(left_short(cov[r, pl.ds(m * COV + e * B, B), :]))
            rhs[e, m] = rhs[e, m] - product_short(z, y)

    def rest_of_block(r, m):
        if r + 2 < NB:
            solve(r, m, r + 2, NB - r - 2)
            update_block(r, m, r + 2, NB - r - 2, r + 1)
            for e in range(r + 2, NB):
                update_block(r, m, e, NB - e, e)
        finish_rhs(r, m)

    for r in range(NB):
        pivot_rows = factor_block(r)
        if r < K:
            solved = [solve(r, m, r + 1, 1) for m in range(slots)]
            for m in range(slots):
                x = left_short(solved[m])
                here = pl.ds(m * COV + (r + 1) * B, B)
                cov[r + 1, here, :] = cov[r + 1, here, :] - product_short(x, right_short(x))
        later_work += [lambda r=r, m=m: rest_of_block(r, m) for m in range(slots)]
        if not DEFER or r == K:
            for work in later_work:
                work()
            later_work.clear()
    dets = pivot_rows[0]
    for t in range(1, B):
        dets = jnp.where(lane == t, pivot_rows[t], dets)
    total = jnp.sum(jnp.log(dets), axis=1, keepdims=True)
    live_count = meta_ref[wide_index]
    for m in range(slots):
        logdet_ref[m] = jnp.where(m < live_count, total[m, 0], 0.0)
    for m in range(slots):
        live = (m < live_count).astype(f32)
        out_ref[m] = rhs[K, m, 0:4, :] * live


def local(coords, fields, counts, place, neighbours):
    slots = coords.shape[0]
    n_wide = lax.axis_size("wide")
    n_tile = lax.axis_size("tile")
    blocks = jnp.concatenate([coords, fields], axis=1)
    prior = lax.ppermute(blocks, "tile", [(i, i + 1) for i in range(n_tile - 1)])
    table = lax.all_gather(jnp.stack([blocks, prior]), "wide", axis=0)
    meta = jnp.concatenate([counts.reshape(-1), place, neighbours.reshape(-1)])
    smem = pl.BlockSpec(memory_space=pltpu.SMEM)
    vmem = pl.BlockSpec(memory_space=pltpu.VMEM)
    return pl.pallas_call(
        lambda *refs: whiten_kernel(n_wide, slots, place.shape[0], *refs),
        out_shape=(
            jax.ShapeDtypeStruct((slots, 4, B), f32),
            jax.ShapeDtypeStruct((slots,), f32),
        ),
        in_specs=[smem, vmem],
        out_specs=(vmem, smem),
        scratch_shapes=[
            pltpu.VMEM((NB, (SUB + 1) * COV, B), f32),
            pltpu.VMEM((2, (SUB + 1) * FACTOR, B), f32),
            pltpu.VMEM((B, B), f32),
            pltpu.VMEM((B, B), f32),
            pltpu.VMEM((NB, slots, SUB, B), f32),
            pltpu.VMEM(((SUB + 1) * SWEEP, B), f32),
            pltpu.VMEM(((SUB + 1) * SWEEP, B), f32),
        ],
        compiler_params=pltpu.CompilerParams(vmem_limit_bytes=48 << 20),
    )(meta, table)


def solution(mesh):
    in_specs = (
        P(("tile", "wide"), None, None),
        P(("tile", "wide"), None, None),
        P("tile", None),
        P(),
        P("tile", None),
    )
    out_specs = (P(("tile", "wide"), None, None), P(("tile", "wide")))
    return jax.shard_map(local, mesh=mesh, in_specs=in_specs, out_specs=out_specs, check_vma=False)
```
